768 devices in a mesh: space: 64 (over y, x, core), tm: 12 (over z).
Axes of the slice: x: 4, y: 8, z: 12, core: 2. Of those that a mesh axis runs over, the one named last changes fastest.
Arguments:
- velocity: bfloat16 [3, 24576, 3072], P(None, 'space', 'tm'), may hold values from -16 to 16
- metric: float32 [24576], P('space'), may hold values from 0.5 to 2
Outputs:
- tiles: float32 [3072, 3072], P('tm', 'space')
The draws below stay inside these ranges and needn't reach their ends.
All inputs are finite; a program needn't handle non-finite values.
Results may differ from the reference program's by a relative error of at most 0.0016.
Values may be sent and summed in bfloat16 or wider, within the bound.
A program may use at most 32 MiB of HBM per device.

```python
import math
import jax
import jax.numpy as jnp
from jax import lax

S = 256
CELLS = 24576
SNAPS = 3072
N_TM = 12


def raised(result, own_key, source, target, shards_of, factor):
    def block_of(axis_at):
        return (jnp.arange(result.shape[axis_at]) // (result.shape[axis_at] // shards_of)).reshape((-1,) + (1,) * (result.ndim - 1 - axis_at))

    first = jax.random.permutation(own_key, shards_of)[block_of(target)]
    second = (block_of(target) + shards_of // 2) % shards_of
    return jnp.where((block_of(source) == first) | (block_of(source) == second), factor * result, result)


def level_of(own_key, extent, cuts, least, high):
    factor_of = 1.0
    for dim, shards_of in cuts:
        draws = jax.random.uniform(jax.random.fold_in(jax.random.fold_in(own_key, 6), dim), (shards_of,), jnp.float32, least / len(cuts), high / len(cuts))
        factor_of = factor_of * jnp.repeat(jnp.exp(draws), extent[dim] // shards_of).reshape((-1,) + (1,) * (len(extent) - 1 - dim))
    return factor_of


def noise_with(rng, dims, spread, reach, pieces, heavy, kind=jnp.bfloat16):
    drawn = spread * jax.random.normal(rng, dims, jnp.float32)
    if pieces:
        drawn = drawn * level_of(rng, dims, pieces, -0.22, 0.18)
    return jnp.clip(raised(drawn, jax.random.fold_in(rng, 3), *heavy), -reach, reach).astype(kind)


def setup_inputs(seed: int = 0) -> dict:
    splits = jax.random.split(jax.random.key(seed), 3)
    return {
        "velocity": noise_with(splits[0], (3, CELLS, SNAPS), 1.0, 16.0, ((1, 64), (2, 12)), (1, 2, 64, 4.0)),
        "metric": jnp.clip(jnp.exp(math.log(2.0) - 1.3862944 * jax.random.uniform(splits[1], (CELLS,), jnp.float32) ** level_of(splits[1], (CELLS,), ((0, 64),), -0.2, 0.2)), 0.5, 2.0),
    }


def features(velocity, metric):
    field = velocity.astype(jnp.float32)
    padded = jnp.pad(field, ((0, 0), (1, 1), (0, 0)))
    gradient = metric[None, :, None] * (padded[:, 2:] - padded[:, :-2]) * 0.5
    helical = gradient[2] + field[0] * gradient[1] - field[1] * gradient[0]
    return jnp.stack([gradient[0], gradient[1], helical]).astype(jnp.bfloat16)

def reference(velocity, metric):
    snapshot_panel = features(velocity, metric)
    flattened = snapshot_panel.reshape(3 * CELLS, SNAPS).astype(jnp.float32)
    shifted = jnp.roll(flattened, -1, axis=1)
    products = jnp.dot(flattened.T.astype(jnp.float32), shifted.astype(jnp.float32), precision=lax.Precision.HIGHEST, preferred_element_type=jnp.float32)
    blocks = flattened.reshape(3 * CELLS, N_TM, S)
    gram_matrix = jnp.einsum('rgs,rgt->gst', blocks, blocks, precision=lax.Precision.HIGHEST)
    factor = jnp.linalg.cholesky(gram_matrix)
    grouped = products.reshape(N_TM, S, SNAPS)
    solved = lax.linalg.triangular_solve(factor, grouped, left_side=True, lower=True)
    return solved.reshape(SNAPS, SNAPS)
```

```python
import jax
import jax.numpy as jnp
from jax import lax
from jax.experimental import pallas as pl
from jax.experimental.pallas import tpu as pltpu
from jax.sharding import PartitionSpec as P

MESH = pl.DeviceIdType.MESH
X, Y, Z = 4, 8, 12
SPACE = 2 * X * Y
S = 256
PAIRS = ((0, 0), (0, 1), (-1, 1), (-1, 2), (-2, 2), (-2, 3), (-3, 3))
LAST = len(PAIRS) - 1
REACH = 3
BLOCK = 32
NT = (((1,), (1,)), ((), ()))
NN = (((1,), (0,)), ((), ()))
F32 = jnp.float32


def exact_dot(left, right, dims):
    return lax.dot_general(
        left, right, dims, precision=lax.Precision.HIGHEST, preferred_element_type=F32
    )


def factor_step(table, j):
    low = j * BLOCK
    rows = table[low : low + BLOCK, :]
    row_at = lax.broadcasted_iota(jnp.int32, (BLOCK, BLOCK), 0)
    lane_at = lax.broadcasted_iota(jnp.int32, (BLOCK, BLOCK), 1)
    eye = jnp.where(row_at == lane_at, 1.0, 0.0).astype(F32)
    work = jnp.concatenate([rows[:, low : low + BLOCK], eye], axis=1)
    below = lax.broadcasted_iota(jnp.int32, work.shape, 0)
    for k in range(BLOCK - 1):
        column = jnp.broadcast_to(work[:, k : k + 1], work.shape)
        pivot = jnp.broadcast_to(column[k : k + 1, :], work.shape)
        pivot_row = jnp.broadcast_to(work[k : k + 1, :], work.shape)
        scale = jnp.where(below > k, column / pivot, 0.0)
        work = work - scale * pivot_row
    pivots = jnp.sum(jnp.where(row_at == lane_at, work[:, :BLOCK], 0.0), axis=1, keepdims=True)
    inverse = work[:, BLOCK:] / jnp.sqrt(pivots)
    solved = exact_dot(inverse, rows, NN)
    table[low : low + BLOCK, :] = solved
    if low + BLOCK < S:
        panel = jnp.transpose(solved[:, :S])[low + BLOCK :, :]
        table[low + BLOCK :, :] = table[low + BLOCK :, :] - exact_dot(panel, solved, NN)


def kernel(
    v_ref, m_ref, out_ref,
    xt, halo, part, cr, cs, xr, xs, yr, ys, gram, table, fin,
    halo_send, halo_recv, z_send, z_recv, c_send, c_recv, x_send, x_recv, y_send, y_recv,
    g_send, g_recv, f_send, f_recv,
):
    s = lax.axis_index("space")
    c = lax.axis_index("tm")
    core = lax.rem(s, 2)
    x = lax.rem(lax.div(s, 2), X)
    y = lax.div(s, 2 * X)
    plus, minus = lax.rem(c + 1, Z), lax.rem(c + Z - 1, Z)
    cells = v_ref.shape[1]

    def at(y_at, x_at, core_at):
        return (y_at * X + x_at) * 2 + core_at

    partner = at(y, x, 1 - core)
    x_peers = [at(y, lax.rem(x + t, X), core) for t in range(1, X)]
    y_peers = [at(lax.rem(y + t, Y), x, core) for t in range(1, Y)]

    barrier = pltpu.get_barrier_semaphore()
    greeted = [(lax.rem(s + 1, SPACE), c), (lax.rem(s + SPACE - 1, SPACE), c), (partner, c), (s, plus), (s, minus)]
    greeted += [(peer, c) for peer in x_peers + y_peers]
    for device in greeted:
        pl.semaphore_signal(barrier, inc=1, device_id=device, device_id_type=MESH)
    pl.semaphore_wait(barrier, len(greeted))

    def remote(src, dst, send, recv, device):
        return pltpu.make_async_remote_copy(
            src_ref=src, dst_ref=dst, send_sem=send, recv_sem=recv, device_id=device, device_id_type=MESH
        )

    def arrived(ref, sem):
        pltpu.make_async_copy(ref, ref, sem).wait()

    to_right = remote(v_ref.at[:, cells - 16 :, :], halo.at[0], halo_send.at[0], halo_recv.at[0], (lax.rem(s + 1, SPACE), c))
    to_left = remote(v_ref.at[:, :16, :], halo.at[1], halo_send.at[1], halo_recv.at[1], (lax.rem(s + SPACE - 1, SPACE), c))

    @pl.when(s < SPACE - 1)
    def _():
        to_right.start()

    @pl.when(s > 0)
    def _():
        to_left.start()
        to_right.wait_recv()

    @pl.when(s == 0)
    def _():
        halo[0] = jnp.zeros_like(halo[0])

    @pl.when(s < SPACE - 1)
    def _():
        to_left.wait_recv()

    @pl.when(s == SPACE - 1)
    def _():
        halo[1] = jnp.zeros_like(halo[1])

    row = lax.broadcasted_iota(jnp.int32, (cells, S), 0)
    spacing = jnp.transpose(jnp.broadcast_to(m_ref[...].reshape(1, cells), (128, cells)))
    spacing = jnp.concatenate([spacing, spacing], axis=1)

    def gradient(k):
        field = v_ref[k].astype(F32)
        first = jnp.broadcast_to(halo[0, k].astype(F32)[15:16, :], (cells, S))
        last = jnp.broadcast_to(halo[1, k].astype(F32)[0:1, :], (cells, S))
        after = jnp.where(row == cells - 1, last, pltpu.roll(field, cells - 1, 0))
        before = jnp.where(row == 0, first, pltpu.roll(field, 1, 0))
        return spacing * (after - before) * 0.5

    def hop(t, comp):
        for way, device, sign in ((0, plus, -1), (1, minus, 1)):
            remote(
                xt.at[REACH + sign * (t - 1), comp], xt.at[REACH + sign * t, comp],
                z_send.at[way], z_recv.at[way, t - 1, comp], (s, device),
            ).start()

    def landed(t, comp):
        for way, sign in ((0, -1), (1, 1)):
            arrived(xt.at[REACH + sign * t, comp], z_recv.at[way, t - 1, comp])

    g0 = gradient(0)
    xt[REACH, 0] = jnp.transpose(g0).astype(jnp.bfloat16)
    hop(1, 0)
    g1 = gradient(1)
    xt[REACH, 1] = jnp.transpose(g1).astype(jnp.bfloat16)
    hop(1, 1)
    g2 = gradient(2) + v_ref[0].astype(F32) * g1 - v_ref[1].astype(F32) * g0
    xt[REACH, 2] = jnp.transpose(g2).astype(jnp.bfloat16)
    hop(1, 2)

    def multiply(p, comps):
        low, high = PAIRS[p]
        for comp in comps:
            lower, upper = xt[REACH + low, comp], xt[REACH + high, comp]
            for side, (left, right) in enumerate(((upper, lower), (lower, upper))):
                if side == 1 and p in (0, LAST):
                    continue
                term = lax.dot_general(left, right, NT, preferred_element_type=F32)
                if comp == 0:
                    part[p, side] = term
                else:
                    part[p, side] = part[p, side] + term

    def on_pair(p, body):
        if p == LAST:
            pl.when(core == 0)(body)
        else:
            body()

    def core_copy(p):
        src = part.at[p, 0] if p in (0, LAST) else part.at[p, 1 - core]
        return remote(src, cr.at[p], c_send.at[p], c_recv.at[p], (partner, c))

    def core_start(p):
        if p == LAST:
            pl.when(core == 1)(lambda: core_copy(p).start())
        else:
            core_copy(p).start()

    def x_start(p):
        def body():
            core_copy(p).wait_recv()
            own = part[p, 0] if p in (0, LAST) else part[p, core]
            cs[p] = own + cr[p]
            for t in range(1, X):
                chunk = pl.ds(pl.multiple_of(lax.rem(x + t, X) * 64, 64), 64)
                remote(cs.at[p, chunk], xr.at[p, t - 1], x_send.at[p], x_recv.at[p], (x_peers[t - 1], c)).start()

        on_pair(p, body)

    def y_start(p):
        def body():
            arrived(xr.at[p], x_recv.at[p])
            xs[p] = cs[p, pl.ds(pl.multiple_of(x * 64, 64), 64)] + xr[p, 0] + xr[p, 1] + xr[p, 2]
            for t in range(1, Y):
                chunk = pl.ds(pl.multiple_of(lax.rem(y + t, Y) * 8, 8), 8)
                remote(xs.at[p, chunk], yr.at[p, t - 1], y_send.at[p], y_recv.at[p], (y_peers[t - 1], c)).start()

        on_pair(p, body)

    def y_finish(p):
        arrived(yr.at[p], y_recv.at[p])
        total = xs[p, pl.ds(pl.multiple_of(y * 8, 8), 8)]
        for t in range(Y - 1):
            total = total + yr[p, t]
        return total

    def gram_y():
        rows = pl.ds(pl.multiple_of(x * 64 + y * 8, 8), 8)
        gram[rows] = y_finish(0)
        for t in range(1, Y):
            remote(gram.at[rows], gram.at[rows], g_send.at[0], g_recv.at[0], (y_peers[t - 1], c)).start()

    def gram_x():
        arrived(yr.at[0], g_recv.at[0])
        rows = pl.ds(pl.multiple_of(x * 64, 64), 64)
        for t in range(1, X):
            remote(gram.at[rows], gram.at[rows], g_send.at[1], g_recv.at[1], (x_peers[t - 1], c)).start()

    def gram_finish():
        arrived(xr.at[0], g_recv.at[1])

    unit = x * Y + y

    def place(p):
        low, high = PAIRS[p]
        lanes_of = jnp.where(core == 0, low, high)
        rows_of = jnp.where(core == 0, high, low)
        group = lax.rem(c + lanes_of + Z, Z)
        number = lax.rem(c + rows_of + Z, Z) * 32 + unit
        owner, slot = lax.div(number, 6), lax.rem(number, 6)
        return group, owner, slot

    def to_owner(p):
        group, owner, slot = place(p)
        rows = pl.ds(pl.multiple_of(slot * 8, 8), 8)
        mine = jnp.logical_and(owner == s, group == c)
        return mine, rows, remote(ys.at[p], fin.at[rows], f_send.at[p, 0], f_recv.at[slot], (owner, group))

    def to_ahead(p):
        group, owner, slot = place(p)
        ahead = lax.rem(owner + SPACE - 1, SPACE)
        mine = jnp.logical_and(ahead == s, group == c)
        return slot == 0, mine, remote(ys.at[p], fin.at[48:56], f_send.at[p, 1], f_recv.at[6], (ahead, group))

    def deliver(p):
        def body():
            ys[p] = y_finish(p)
            mine, rows, copy = to_owner(p)

            @pl.when(mine)
            def _():
                fin[rows] = ys[p]

            @pl.when(jnp.logical_not(mine))
            def _():
                copy.start()

            first, mine_ahead, copy_ahead = to_ahead(p)

            @pl.when(jnp.logical_and(first, mine_ahead))
            def _():
                fin[48:56] = ys[p]

            @pl.when(jnp.logical_and(first, jnp.logical_not(mine_ahead)))
            def _():
                copy_ahead.start()

        on_pair(p, body)

    def sent(p):
        def body():
            mine, _, copy = to_owner(p)

            @pl.when(jnp.logical_not(mine))
            def _():
                copy.wait_send()

            first, mine_ahead, copy_ahead = to_ahead(p)

            @pl.when(jnp.logical_and(first, jnp.logical_not(mine_ahead)))
            def _():
                copy_ahead.wait_send()

        on_pair(p, body)

    def collect(slot):
        number = lax.rem(s * 6 + slot, SPACE * 6)
        apart = lax.rem(lax.div(number, 32) - c + Z, Z)
        within = lax.rem(number, 32)
        near = apart <= Z // 2
        home = jnp.where(near, lax.div(apart, 2), Z - lax.div(Z - apart + 1, 2))
        source = at(lax.rem(within, Y), lax.div(within, Y), jnp.where(near, 0, 1))
        own = jnp.logical_and(source == s, lax.rem(home, Z) == 0)
        rows = slice(slot * 8, slot * 8 + 8)

        @pl.when(apart == 0)
        def _():
            fin[rows] = gram[pl.ds(pl.multiple_of(within * 8, 8), 8)]

        @pl.when(jnp.logical_and(apart != 0, jnp.logical_not(own)))
        def _():
            arrived(fin.at[rows], f_recv.at[slot])

    everything = range(3)
    multiply(0, everything)
    core_start(0)
    x_start(0)
    landed(1, 0)
    hop(2, 0)
    y_start(0)
    gram_y()
    gram_x()
    landed(1, 1)
    hop(2, 1)
    gram_finish()
    table[:, :S] = gram[...]
    square = (S, S)
    table[:, S:] = jnp.where(
        lax.broadcasted_iota(jnp.int32, square, 0) == lax.broadcasted_iota(jnp.int32, square, 1), 1.0, 0.0
    ).astype(F32)
    factor_step(table, 0)
    landed(1, 2)
    hop(2, 2)
    multiply(1, everything)
    core_start(1)
    multiply(2, everything)
    core_start(2)
    factor_step(table, 1)
    x_start(1)
    x_start(2)
    landed(2, 0)
    hop(3, 0)
    factor_step(table, 2)
    y_start(1)
    y_start(2)
    factor_step(table, 3)
    landed(2, 1)
    hop(3, 1)
    deliver(1)
    deliver(2)
    factor_step(table, 4)
    landed(2, 2)
    hop(3, 2)
    multiply(3, everything)
    core_start(3)
    multiply(4, everything)
    core_start(4)
    factor_step(table, 5)
    x_start(3)
    x_start(4)
    factor_step(table, 6)
    y_start(3)
    y_start(4)
    factor_step(table, 7)
    deliver(3)
    deliver(4)
    for comp in range(3):
        landed(3, comp)
        multiply(5, (comp,))
        multiply(6, (comp,))
    core_start(5)
    core_start(6)
    x_start(5)
    x_start(6)
    y_start(5)
    y_start(6)
    deliver(5)
    deliver(6)
    for slot in range(7):
        collect(slot)
    out_ref[...] = exact_dot(table[:, S:], fin[1:49], NT)

    @pl.when(s < SPACE - 1)
    def _():
        to_right.wait_send()

    @pl.when(s > 0)
    def _():
        to_left.wait_send()

    for way in range(2):
        arrived(xt.at[0:REACH], z_send.at[way])
    arrived(yr.at[0], g_send.at[0])
    arrived(xr.at[0], g_send.at[1])
    for p in range(LAST + 1):
        if p == LAST:
            pl.when(core == 1)(lambda: core_copy(LAST).wait_send())
        else:
            core_copy(p).wait_send()

        def rest(p=p):
            arrived(xr.at[p], x_send.at[p])
            arrived(yr.at[p], y_send.at[p])

        on_pair(p, rest)
        if p > 0:
            sent(p)


def body(velocity, metric):
    cells, pairs = velocity.shape[1], len(PAIRS)
    dma = pltpu.SemaphoreType.DMA
    return pl.pallas_call(
        kernel,
        out_shape=jax.ShapeDtypeStruct((S, 3072 // SPACE), F32),
        in_specs=[pl.BlockSpec(memory_space=pltpu.VMEM)] * 2,
        out_specs=pl.BlockSpec(memory_space=pltpu.VMEM),
        scratch_shapes=[
            pltpu.VMEM((2 * REACH + 1, 3, S, cells), jnp.bfloat16),
            pltpu.VMEM((2, 3, 16, S), jnp.bfloat16),
            pltpu.VMEM((pairs, 2, S, S), F32),
            pltpu.VMEM((pairs, S, S), F32),
            pltpu.VMEM((pairs, S, S), F32),
            pltpu.VMEM((pairs, X - 1, S // X, S), F32),
            pltpu.VMEM((pairs, S // X, S), F32),
            pltpu.VMEM((pairs, Y - 1, 8, S), F32),
            pltpu.VMEM((pairs, 8, S), F32),
            pltpu.VMEM((S, S), F32),
            pltpu.VMEM((S, 2 * S), F32),
            pltpu.VMEM((56, S), F32),
            dma((2,)), dma((2,)), dma((2,)), dma((2, REACH, 3)),
            dma((pairs,)), dma((pairs,)), dma((pairs,)), dma((pairs,)), dma((pairs,)), dma((pairs,)),
            dma((2,)), dma((2,)), dma((pairs, 2)), dma((7,)),
        ],
        compiler_params=pltpu.CompilerParams(
            collective_id=0, has_side_effects=True, vmem_limit_bytes=48 * 1024 * 1024
        ),
    )(velocity, metric)


def solution(mesh):
    in_specs = (P(None, "space", "tm"), P("space"))
    out_specs = P("tm", "space")
    return jax.shard_map(body, mesh=mesh, in_specs=in_specs, out_specs=out_specs, check_vma=False)
```

```python
import jax
import jax.numpy as jnp
from jax import lax
from jax.experimental import pallas as pl
from jax.experimental.pallas import tpu as pltpu
from jax.sharding import PartitionSpec as P

MESH = pl.DeviceIdType.MESH
X, Y, Z = 4, 8, 12
SPACE = 2 * X * Y
S = 256
PAIRS = ((0, 0), (0, 1), (-1, 1), (-1, 2), (-2, 2), (-2, 3), (-3, 3))
LAST = len(PAIRS) - 1
REACH = 3
THIRD = 128
ORDER = (1, 0, 2)
BLOCK = 64
WIDTH = 8
NT = (((1,), (1,)), ((), ()))
NN = (((1,), (0,)), ((), ()))
F32 = jnp.float32


def exact_dot(left, right, dims):
    return lax.dot_general(
        left, right, dims, precision=lax.Precision.HIGHEST, preferred_element_type=F32
    )


def eliminate(work):
    below = lax.broadcasted_iota(jnp.int32, work.shape, 0)
    for first in range(0, BLOCK, WIDTH):
        columns = [jnp.broadcast_to(work[:, k : k + 1], work.shape) for k in range(first, first + WIDTH)]
        rows = [work[k : k + 1, :] for k in range(first, first + WIDTH)]
        scales = []
        for t in range(WIDTH):
            k = first + t
            scale = jnp.where(below > k, columns[t] * (1.0 / columns[t][k : k + 1, :]), 0.0)
            scales.append(scale)
            for u in range(t + 1, WIDTH):
                columns[u] = columns[u] - scale * columns[u][k : k + 1, :]
                rows[u] = rows[u] - scale[first + u : first + u + 1, :] * rows[t]
        for scale, pivot_row in zip(scales, rows):
            work = work - scale * pivot_row
    return work


def factor_step(table, j):
    low = j * BLOCK
    rows = table[low : low + BLOCK, :]
    row_at = lax.broadcasted_iota(jnp.int32, (BLOCK, BLOCK), 0)
    lane_at = lax.broadcasted_iota(jnp.int32, (BLOCK, BLOCK), 1)
    eye = jnp.where(row_at == lane_at, 1.0, 0.0).astype(F32)
    work = eliminate(jnp.concatenate([rows[:, low : low + BLOCK], eye], axis=1))
    pivots = jnp.sum(jnp.where(row_at == lane_at, work[:, :BLOCK], 0.0), axis=1, keepdims=True)
    inverse = work[:, BLOCK:] / jnp.sqrt(pivots)
    solved = exact_dot(inverse, rows, NN)
    table[low : low + BLOCK, :] = solved
    if low + BLOCK < S:
        panel = jnp.transpose(solved[:, :S])[low + BLOCK :, :]
        table[low + BLOCK :, :] = table[low + BLOCK :, :] - exact_dot(panel, solved, NN)


def kernel(
    v_hbm, m_hbm, out_ref,
    v_ref, m_ref, xt, halo, part, cr, cs, xr, xs, yr, ys, last_yr, last_s, last_xr, gram, table, fin,
    in_sem, halo_send, halo_recv, z_send, z_recv, c_send, c_recv, x_send, x_recv, y_send, y_recv,
    g_send, g_recv, f_send, f_recv,
):
    s = lax.axis_index("space")
    c = lax.axis_index("tm")
    core = lax.rem(s, 2)
    x = lax.rem(lax.div(s, 2), X)
    y = lax.div(s, 2 * X)
    plus, minus = lax.rem(c + 1, Z), lax.rem(c + Z - 1, Z)
    right, left = lax.rem(s + 1, SPACE), lax.rem(s + SPACE - 1, SPACE)
    cells = v_ref.shape[1]

    def at(y_at, x_at, core_at):
        return (y_at * X + x_at) * 2 + core_at

    partner = at(y, x, 1 - core)
    x_peers = [at(y, lax.rem(x + t, X), core) for t in range(X)]
    y_peers = [at(lax.rem(y + t, Y), x, core) for t in range(Y)]

    barrier = pltpu.get_barrier_semaphore()
    greeted = [(s, plus), (s, minus), (right, c), (left, c), (partner, c)]
    greeted += [(peer, c) for peer in x_peers[1:] + y_peers[1:]]
    for device in greeted:
        pl.semaphore_signal(barrier, inc=1, device_id=device, device_id_type=MESH)
    fetch_v = pltpu.make_async_copy(v_hbm, v_ref, in_sem.at[0])
    fetch_m = pltpu.make_async_copy(m_hbm, m_ref, in_sem.at[1])
    fetch_v.start()
    fetch_m.start()
    fetch_v.wait()
    fetch_m.wait()
    pl.semaphore_wait(barrier, len(greeted))

    def remote(src, dst, send, recv, device):
        return pltpu.make_async_remote_copy(
            src_ref=src, dst_ref=dst, send_sem=send, recv_sem=recv, device_id=device, device_id_type=MESH
        )

    def arrived(ref, sem):
        pltpu.make_async_copy(ref, ref, sem).wait()

    to_right = remote(v_ref.at[:, cells - 16 :, :], halo.at[0], halo_send.at[0], halo_recv.at[0], (right, c))
    to_left = remote(v_ref.at[:, :16, :], halo.at[1], halo_send.at[1], halo_recv.at[1], (left, c))

    @pl.when(s < SPACE - 1)
    def _():
        to_right.start()

    @pl.when(s > 0)
    def _():
        to_left.start()

    def halo_landed():
        @pl.when(s > 0)
        def _():
            to_right.wait_recv()

        @pl.when(s == 0)
        def _():
            halo[0] = jnp.zeros_like(halo[0])

        @pl.when(s < SPACE - 1)
        def _():
            to_left.wait_recv()

        @pl.when(s == SPACE - 1)
        def _():
            halo[1] = jnp.zeros_like(halo[1])

    row = lax.broadcasted_iota(jnp.int32, (THIRD, S), 0)

    def features(q):
        low = q * THIRD
        start, stop = max(low - 16, 0), min(low + THIRD + 16, cells)
        here = slice(low - start, low - start + THIRD)
        spacing = jnp.transpose(jnp.broadcast_to(m_ref[low : low + THIRD].reshape(1, THIRD), (THIRD, THIRD)))
        spacing = jnp.concatenate([spacing, spacing], axis=1)
        gradients = []
        for k in range(3):
            field = v_ref[k, start:stop].astype(F32)
            after = pltpu.roll(field, stop - start - 1, 0)[here]
            before = pltpu.roll(field, 1, 0)[here]
            if stop == cells:
                edge = jnp.broadcast_to(halo[1, k].astype(F32)[0:1, :], (THIRD, S))
                after = jnp.where(row == THIRD - 1, edge, after)
            if start == 0:
                edge = jnp.broadcast_to(halo[0, k].astype(F32)[15:16, :], (THIRD, S))
                before = jnp.where(row == 0, edge, before)
            gradients.append(spacing * (after - before) * 0.5)
        center = [v_ref[k, low : low + THIRD].astype(F32) for k in range(2)]
        gradients[2] = gradients[2] + center[0] * gradients[1] - center[1] * gradients[0]
        for k in range(3):
            xt[REACH, q, :, k * THIRD : (k + 1) * THIRD] = jnp.transpose(gradients[k]).astype(jnp.bfloat16)

    def hop(t, q):
        for way, device, sign in ((0, plus, -1), (1, minus, 1)):
            remote(
                xt.at[REACH + sign * (t - 1), q], xt.at[REACH + sign * t, q],
                z_send.at[way], z_recv.at[way, t - 1, q], (s, device),
            ).start()

    def landed(t, q):
        for way, sign in ((0, -1), (1, 1)):
            arrived(xt.at[REACH + sign * t, q], z_recv.at[way, t - 1, q])

    def multiply(p, thirds):
        low, high = PAIRS[p]
        for q in thirds:
            lower, upper = xt[REACH + low, q], xt[REACH + high, q]
            for side, (one, other) in enumerate(((upper, lower), (lower, upper))):
                if side == 1 and p in (0, LAST):
                    continue
                term = lax.dot_general(one, other, NT, preferred_element_type=F32)
                if q == ORDER[0]:
                    part[p, side] = term
                else:
                    part[p, side] = part[p, side] + term

    def on_pair(p, body):
        if p == LAST:
            pl.when(core == 0)(body)
        else:
            body()

    def stages(p):
        x_axis = (x, x_peers, X, x_send.at[p], x_recv.at[p])
        y_axis = (y, y_peers, Y, y_send.at[p], y_recv.at[p])
        if p == LAST:
            return (y_axis, last_yr, last_s, S // Y), (x_axis, last_xr, last_s, 8)
        return (x_axis, xr.at[p], xs.at[p], S // X), (y_axis, yr.at[p], xs.at[p], 8)

    def piece(p, t):
        (at_axis, _, count, _, _), _, _, size = stages(p)[0]
        return pl.ds(pl.multiple_of(lax.rem(at_axis + t, count) * size, size), size)

    def core_copy(p, t):
        side = 0 if p in (0, LAST) else 1 - core
        rows = piece(p, t)
        return remote(part.at[p, side, rows], cr.at[p, rows], c_send.at[p], c_recv.at[p, t], (partner, c))

    def core_start(p):
        def body():
            for t in order(p):
                core_copy(p, t).start()

        if p == LAST:
            pl.when(core == 1)(body)
        else:
            body()

    def order(p):
        count = stages(p)[0][0][2]
        return tuple(range(1, count)) + (0,)

    def first_stage(p):
        (_, peers, _, send, recv), landing, _, _ = stages(p)[0]

        def body():
            for t in order(p):
                core_copy(p, t).wait_recv()
                rows = piece(p, t)
                own = part[p, 0, rows] if p in (0, LAST) else part[p, core, rows]
                cs[p, rows] = own + cr[p, rows]
                if t > 0:
                    remote(cs.at[p, rows], landing.at[t - 1], send, recv, (peers[t], c)).start()

        on_pair(p, body)

    def second_stage(p):
        (_, _, count, _, recv), landing, summed, _ = stages(p)[0]
        (at_axis, peers, others, send, recv_next), landing_next, _, size = stages(p)[1]

        def body():
            arrived(landing, recv)
            total = cs[p, piece(p, 0)]
            for t in range(count - 1):
                total = total + landing[t]
            summed[...] = total
            for t in range(1, others):
                chunk = pl.ds(pl.multiple_of(lax.rem(at_axis + t, others) * size, size), size)
                remote(summed.at[chunk], landing_next.at[t - 1], send, recv_next, (peers[t], c)).start()

        on_pair(p, body)

    def finish(p):
        (at_axis, _, count, _, recv), landing, summed, size = stages(p)[1]
        arrived(landing, recv)
        total = summed[pl.ds(pl.multiple_of(at_axis * size, size), size)]
        for t in range(count - 1):
            total = total + landing[t]
        return total

    def gram_y():
        rows = pl.ds(pl.multiple_of(x * 64 + y * 8, 8), 8)
        gram[rows] = finish(0)
        for t in range(1, Y):
            remote(gram.at[rows], gram.at[rows], g_send.at[0], g_recv.at[0], (y_peers[t], c)).start()

    def gram_x():
        arrived(yr.at[0], g_recv.at[0])
        rows = pl.ds(pl.multiple_of(x * 64, 64), 64)
        for t in range(1, X):
            remote(gram.at[rows], gram.at[rows], g_send.at[1], g_recv.at[1], (x_peers[t], c)).start()

    def gram_finish():
        arrived(xr.at[0], g_recv.at[1])
        table[:, :S] = gram[...]
        square = (S, S)
        table[:, S:] = jnp.where(
            lax.broadcasted_iota(jnp.int32, square, 0) == lax.broadcasted_iota(jnp.int32, square, 1), 1.0, 0.0
        ).astype(F32)

    def place(p):
        low, high = PAIRS[p]
        unit = y * X + x if p == LAST else x * Y + y
        lanes_of = jnp.where(core == 0, low, high)
        rows_of = jnp.where(core == 0, high, low)
        group = lax.rem(c + lanes_of + Z, Z)
        number = lax.rem(c + rows_of + Z, Z) * 32 + unit
        owner, slot = lax.div(number, 6), lax.rem(number, 6)
        return group, owner, slot

    def to_owner(p):
        group, owner, slot = place(p)
        rows = pl.ds(pl.multiple_of(slot * 8, 8), 8)
        mine = jnp.logical_and(owner == s, group == c)
        return mine, rows, remote(ys.at[p], fin.at[rows], f_send.at[p, 0], f_recv.at[slot], (owner, group))

    def to_ahead(p):
        group, owner, slot = place(p)
        ahead = lax.rem(owner + SPACE - 1, SPACE)
        mine = jnp.logical_and(ahead == s, group == c)
        return slot == 0, mine, remote(ys.at[p], fin.at[48:56], f_send.at[p, 1], f_recv.at[6], (ahead, group))

    def deliver(p):
        def body():
            ys[p] = finish(p)
            mine, rows, copy = to_owner(p)

            @pl.when(mine)
            def _():
                fin[rows] = ys[p]

            @pl.when(jnp.logical_not(mine))
            def _():
                copy.start()

            first, mine_ahead, copy_ahead = to_ahead(p)

            @pl.when(jnp.logical_and(first, mine_ahead))
            def _():
                fin[48:56] = ys[p]

            @pl.when(jnp.logical_and(first, jnp.logical_not(mine_ahead)))
            def _():
                copy_ahead.start()

        on_pair(p, body)

    def sent(p):
        def body():
            mine, _, copy = to_owner(p)

            @pl.when(jnp.logical_not(mine))
            def _():
                copy.wait_send()

            first, mine_ahead, copy_ahead = to_ahead(p)

            @pl.when(jnp.logical_and(first, jnp.logical_not(mine_ahead)))
            def _():
                copy_ahead.wait_send()

        on_pair(p, body)

    def collect(slot):
        number = lax.rem(s * 6 + slot, SPACE * 6)
        apart = lax.rem(lax.div(number, 32) - c + Z, Z)
        within = lax.rem(number, 32)
        near = apart <= Z // 2
        home = jnp.where(near, lax.div(apart, 2), Z - lax.div(Z - apart + 1, 2))
        y_at = jnp.where(apart == Z // 2, lax.div(within, X), lax.rem(within, Y))
        x_at = jnp.where(apart == Z // 2, lax.rem(within, X), lax.div(within, Y))
        source = at(y_at, x_at, jnp.where(near, 0, 1))
        own = jnp.logical_and(source == s, lax.rem(home, Z) == 0)
        rows = slice(slot * 8, slot * 8 + 8)

        @pl.when(apart == 0)
        def _():
            fin[rows] = gram[pl.ds(pl.multiple_of(within * 8, 8), 8)]

        @pl.when(jnp.logical_and(apart != 0, jnp.logical_not(own)))
        def _():
            arrived(fin.at[rows], f_recv.at[slot])

    one, two, three = ORDER
    features(one)
    hop(1, one)
    halo_landed()
    features(two)
    hop(1, two)
    features(three)
    hop(1, three)
    multiply(0, ORDER)
    core_start(0)
    landed(1, one)
    hop(2, one)
    first_stage(0)
    landed(1, two)
    hop(2, two)
    second_stage(0)
    landed(1, three)
    hop(2, three)
    gram_y()
    for p in (1, 2):
        multiply(p, ORDER)
        core_start(p)
    landed(2, one)
    hop(3, one)
    gram_x()
    first_stage(1)
    first_stage(2)
    landed(2, two)
    hop(3, two)
    gram_finish()
    factor_step(table, 0)
    second_stage(1)
    second_stage(2)
    landed(2, three)
    hop(3, three)
    for p in (3, 4):
        multiply(p, ORDER)
        core_start(p)
    factor_step(table, 1)
    deliver(1)
    deliver(2)
    landed(3, one)
    multiply(5, (one,))
    multiply(6, (one,))
    first_stage(3)
    first_stage(4)
    factor_step(table, 2)
    landed(3, two)
    multiply(5, (two,))
    multiply(6, (two,))
    second_stage(3)
    second_stage(4)
    landed(3, three)
    multiply(5, (three,))
    core_start(5)
    multiply(6, (three,))
    core_start(6)
    factor_step(table, 3)
    first_stage(5)
    first_stage(6)
    deliver(3)
    deliver(4)
    second_stage(5)
    second_stage(6)
    deliver(5)
    deliver(6)
    for slot in range(7):
        collect(slot)
    out_ref[...] = exact_dot(fin[1:49], table[:, S:], NT)

    @pl.when(s < SPACE - 1)
    def _():
        to_right.wait_send()

    @pl.when(s > 0)
    def _():
        to_left.wait_send()

    for way in range(2):
        arrived(xt.at[0:REACH], z_send.at[way])
    arrived(yr.at[0], g_send.at[0])
    arrived(xr.at[0], g_send.at[1])
    for p in range(LAST + 1):
        if p == LAST:
            pl.when(core == 1)(lambda: arrived(cr.at[LAST], c_send.at[LAST]))
        else:
            arrived(cr.at[p], c_send.at[p])

        def rest(p=p):
            for (_, _, _, send, _), landing, _, _ in stages(p):
                arrived(landing, send)

        on_pair(p, rest)
        if p > 0:
            sent(p)


def body(velocity, metric):
    cells, pairs = velocity.shape[1], len(PAIRS)
    dma = pltpu.SemaphoreType.DMA
    tiles = pl.pallas_call(
        kernel,
        out_shape=jax.ShapeDtypeStruct((3072 // SPACE, S), F32),
        in_specs=[pl.BlockSpec(memory_space=pl.ANY)] * 2,
        out_specs=pl.BlockSpec(memory_space=pltpu.VMEM),
        scratch_shapes=[
            pltpu.VMEM((3, cells, S), jnp.bfloat16),
            pltpu.VMEM((cells,), F32),
            pltpu.VMEM((2 * REACH + 1, 3, S, cells), jnp.bfloat16),
            pltpu.VMEM((2, 3, 16, S), jnp.bfloat16),
            pltpu.VMEM((pairs, 2, S, S), F32),
            pltpu.VMEM((pairs, S, S), F32),
            pltpu.VMEM((pairs, S, S), F32),
            pltpu.VMEM((pairs - 1, X - 1, S // X, S), F32),
            pltpu.VMEM((pairs - 1, S // X, S), F32),
            pltpu.VMEM((pairs - 1, Y - 1, 8, S), F32),
            pltpu.VMEM((pairs, 8, S), F32),
            pltpu.VMEM((Y - 1, S // Y, S), F32),
            pltpu.VMEM((S // Y, S), F32),
            pltpu.VMEM((X - 1, 8, S), F32),
            pltpu.VMEM((S, S), F32),
            pltpu.VMEM((S, 2 * S), F32),
            pltpu.VMEM((56, S), F32),
            dma((2,)), dma((2,)), dma((2,)), dma((2,)), dma((2, REACH, 3)),
            dma((pairs,)), dma((pairs, Y)), dma((pairs,)), dma((pairs,)), dma((pairs,)), dma((pairs,)),
            dma((2,)), dma((2,)), dma((pairs, 2)), dma((7,)),
        ],
        compiler_params=pltpu.CompilerParams(
            collective_id=0, has_side_effects=True, vmem_limit_bytes=56 * 1024 * 1024
        ),
    )(velocity, metric)
    return tiles.T


def solution(mesh):
    in_specs = (P(None, "space", "tm"), P("space"))
    out_specs = P("tm", "space")
    return jax.shard_map(body, mesh=mesh, in_specs=in_specs, out_specs=out_specs, check_vma=False)
```

```python
import jax
import jax.numpy as jnp
from jax import lax
from jax.experimental import pallas as pl
from jax.experimental.pallas import tpu as pltpu
from jax.sharding import PartitionSpec as P

MESH = pl.DeviceIdType.MESH
X, Y, Z = 4, 8, 12
SPACE = 2 * X * Y
S = 256
PAIRS = ((0, 0), (0, 1), (-1, 1), (-1, 2), (-2, 2), (-2, 3), (-3, 3))
LAST = len(PAIRS) - 1
REACH = 3
THIRD = 128
HALF = S // 2
ORDER = (1, 0, 2)
BLOCK = 64
WIDTH = 8
NT = (((1,), (1,)), ((), ()))
NN = (((1,), (0,)), ((), ()))
F32 = jnp.float32


def exact_dot(left, right, dims):
    return lax.dot_general(
        left, right, dims, precision=lax.Precision.HIGHEST, preferred_element_type=F32
    )


def eliminate(work):
    below = lax.broadcasted_iota(jnp.int32, work.shape, 0)
    for first in range(0, BLOCK, WIDTH):
        columns = [jnp.broadcast_to(work[:, k : k + 1], work.shape) for k in range(first, first + WIDTH)]
        rows = [work[k : k + 1, :] for k in range(first, first + WIDTH)]
        scales = []
        for t in range(WIDTH):
            k = first + t
            scale = jnp.where(below > k, columns[t] * (1.0 / columns[t][k : k + 1, :]), 0.0)
            scales.append(scale)
            for u in range(t + 1, WIDTH):
                columns[u] = columns[u] - scale * columns[u][k : k + 1, :]
                rows[u] = rows[u] - scale[first + u : first + u + 1, :] * rows[t]
        for scale, pivot_row in zip(scales, rows):
            work = work - scale * pivot_row
    return work


def factor_step(table, j):
    low = j * BLOCK
    rows = table[low : low + BLOCK, :]
    row_at = lax.broadcasted_iota(jnp.int32, (BLOCK, BLOCK), 0)
    lane_at = lax.broadcasted_iota(jnp.int32, (BLOCK, BLOCK), 1)
    eye = jnp.where(row_at == lane_at, 1.0, 0.0).astype(F32)
    work = eliminate(jnp.concatenate([rows[:, low : low + BLOCK], eye], axis=1))
    pivots = jnp.sum(jnp.where(row_at == lane_at, work[:, :BLOCK], 0.0), axis=1, keepdims=True)
    inverse = work[:, BLOCK:] / jnp.sqrt(pivots)
    solved = exact_dot(inverse, rows, NN)
    table[low : low + BLOCK, :] = solved
    if low + BLOCK < S:
        panel = jnp.transpose(solved[:, :S])[low + BLOCK :, :]
        table[low + BLOCK :, :] = table[low + BLOCK :, :] - exact_dot(panel, solved, NN)


def kernel(
    v_hbm, m_hbm, out_ref,
    v_ref, m_ref, xt, halo, part, cr, cs, xr, xs, yr, ys,
    last_part, last_cr, last_cs, last_yr, last_s, last_xr, last_ys, gram, table, fin,
    in_sem, halo_send, halo_recv, z_send, z_recv, c_send, c_recv, x_send, x_recv, y_send, y_recv,
    g_send, g_recv, f_send, f_recv,
):
    s = lax.axis_index("space")
    c = lax.axis_index("tm")
    core = lax.rem(s, 2)
    x = lax.rem(lax.div(s, 2), X)
    y = lax.div(s, 2 * X)
    plus, minus = lax.rem(c + 1, Z), lax.rem(c + Z - 1, Z)
    right, left = lax.rem(s + 1, SPACE), lax.rem(s + SPACE - 1, SPACE)
    cells = v_ref.shape[1]

    def at(y_at, x_at, core_at):
        return (y_at * X + x_at) * 2 + core_at

    partner = at(y, x, 1 - core)
    x_peers = [at(y, lax.rem(x + t, X), core) for t in range(X)]
    y_peers = [at(lax.rem(y + t, Y), x, core) for t in range(Y)]

    barrier = pltpu.get_barrier_semaphore()
    greeted = [(s, plus), (s, minus), (right, c), (left, c), (partner, c)]
    greeted += [(peer, c) for peer in x_peers[1:] + y_peers[1:]]
    for device in greeted:
        pl.semaphore_signal(barrier, inc=1, device_id=device, device_id_type=MESH)
    fetch_v = pltpu.make_async_copy(v_hbm, v_ref, in_sem.at[0])
    fetch_m = pltpu.make_async_copy(m_hbm, m_ref, in_sem.at[1])
    fetch_v.start()
    fetch_m.start()
    fetch_v.wait()
    fetch_m.wait()

    def remote(src, dst, send, recv, device):
        return pltpu.make_async_remote_copy(
            src_ref=src, dst_ref=dst, send_sem=send, recv_sem=recv, device_id=device, device_id_type=MESH
        )

    def arrived(ref, sem):
        pltpu.make_async_copy(ref, ref, sem).wait()

    to_right = remote(v_ref.at[:, cells - 16 :, :], halo.at[0], halo_send.at[0], halo_recv.at[0], (right, c))
    to_left = remote(v_ref.at[:, :16, :], halo.at[1], halo_send.at[1], halo_recv.at[1], (left, c))

    def enter():
        pl.semaphore_wait(barrier, len(greeted))

        @pl.when(s < SPACE - 1)
        def _():
            to_right.start()

        @pl.when(s > 0)
        def _():
            to_left.start()

    def halo_landed():
        @pl.when(s > 0)
        def _():
            to_right.wait_recv()

        @pl.when(s == 0)
        def _():
            halo[0] = jnp.zeros_like(halo[0])

        @pl.when(s < SPACE - 1)
        def _():
            to_left.wait_recv()

        @pl.when(s == SPACE - 1)
        def _():
            halo[1] = jnp.zeros_like(halo[1])

    row = lax.broadcasted_iota(jnp.int32, (THIRD, S), 0)

    def features(q):
        low = q * THIRD
        start, stop = max(low - 16, 0), min(low + THIRD + 16, cells)
        here = slice(low - start, low - start + THIRD)
        spacing = jnp.transpose(jnp.broadcast_to(m_ref[low : low + THIRD].reshape(1, THIRD), (THIRD, THIRD)))
        spacing = jnp.concatenate([spacing, spacing], axis=1)
        gradients = []
        for k in range(3):
            field = v_ref[k, start:stop].astype(F32)
            after = pltpu.roll(field, stop - start - 1, 0)[here]
            before = pltpu.roll(field, 1, 0)[here]
            if stop == cells:
                edge = jnp.broadcast_to(halo[1, k].astype(F32)[0:1, :], (THIRD, S))
                after = jnp.where(row == THIRD - 1, edge, after)
            if start == 0:
                edge = jnp.broadcast_to(halo[0, k].astype(F32)[15:16, :], (THIRD, S))
                before = jnp.where(row == 0, edge, before)
            gradients.append(spacing * (after - before) * 0.5)
        center = [v_ref[k, low : low + THIRD].astype(F32) for k in range(2)]
        gradients[2] = gradients[2] + center[0] * gradients[1] - center[1] * gradients[0]
        for k in range(3):
            xt[REACH, q, :, k * THIRD : (k + 1) * THIRD] = jnp.transpose(gradients[k]).astype(jnp.bfloat16)

    def hop(t, q):
        for way, device, sign in ((0, plus, -1), (1, minus, 1)):
            remote(
                xt.at[REACH + sign * (t - 1), q], xt.at[REACH + sign * t, q],
                z_send.at[way], z_recv.at[way, t - 1, q], (s, device),
            ).start()

    def landed(t, q):
        for way, sign in ((0, -1), (1, 1)):
            arrived(xt.at[REACH + sign * t, q], z_recv.at[way, t - 1, q])

    def gather(ref, at_index, term, q):
        ref[at_index] = term if q == ORDER[0] else ref[at_index] + term

    def multiply(p, thirds):
        low, high = PAIRS[p]
        for q in thirds:
            lower, upper = xt[REACH + low, q], xt[REACH + high, q]
            term = lax.dot_general(upper, lower, NT, preferred_element_type=F32)
            if p == LAST:
                gather(last_part, 0, term[:, :HALF], q)
                gather(last_part, 1, term[:, HALF:], q)
                continue
            gather(part, (p, 0), term, q)
            if p > 0:
                gather(part, (p, 1), lax.dot_general(lower, upper, NT, preferred_element_type=F32), q)

    def stages(p):
        x_axis = (x, x_peers, X, x_send.at[p], x_recv.at[p])
        y_axis = (y, y_peers, Y, y_send.at[p], y_recv.at[p])
        if p == LAST:
            return (y_axis, last_yr, last_s, S // Y), (x_axis, last_xr, last_s, 8)
        return (x_axis, xr.at[p], xs.at[p], S // X), (y_axis, yr.at[p], xs.at[p], 8)

    def core_refs(p):
        if p == LAST:
            return last_part.at[core], last_part.at[1 - core], last_cr, last_cs
        if p == 0:
            return part.at[0, 0], part.at[0, 0], cr.at[0], cs.at[0]
        return part.at[p, core], part.at[p, 1 - core], cr.at[p], cs.at[p]

    def piece(p, t):
        (at_axis, _, count, _, _), _, _, size = stages(p)[0]
        return pl.ds(pl.multiple_of(lax.rem(at_axis + t, count) * size, size), size)

    def order(p):
        count = stages(p)[0][0][2]
        return tuple(range(1, count)) + (0,)

    def core_copy(p, t):
        _, given, landing, _ = core_refs(p)
        rows = piece(p, t)
        return remote(given.at[rows], landing.at[rows], c_send.at[p], c_recv.at[p, t], (partner, c))

    def core_start(p):
        for t in order(p):
            core_copy(p, t).start()

    def first_stage(p):
        (_, peers, _, send, recv), landing, _, _ = stages(p)[0]
        kept, _, received, summed = core_refs(p)
        for t in order(p):
            core_copy(p, t).wait_recv()
            rows = piece(p, t)
            summed[rows] = kept[rows] + received[rows]
            if t > 0:
                remote(summed.at[rows], landing.at[t - 1], send, recv, (peers[t], c)).start()

    def second_stage(p):
        (_, _, count, _, recv), landing, summed, _ = stages(p)[0]
        (at_axis, peers, others, send, recv_next), landing_next, _, size = stages(p)[1]
        arrived(landing, recv)
        total = core_refs(p)[3][piece(p, 0)]
        for t in range(count - 1):
            total = total + landing[t]
        summed[...] = total
        for t in range(1, others):
            chunk = pl.ds(pl.multiple_of(lax.rem(at_axis + t, others) * size, size), size)
            remote(summed.at[chunk], landing_next.at[t - 1], send, recv_next, (peers[t], c)).start()

    def finish(p):
        (at_axis, _, count, _, recv), landing, summed, size = stages(p)[1]
        arrived(landing, recv)
        total = summed[pl.ds(pl.multiple_of(at_axis * size, size), size)]
        for t in range(count - 1):
            total = total + landing[t]
        return total

    def gram_y():
        rows = pl.ds(pl.multiple_of(x * 64 + y * 8, 8), 8)
        gram[rows] = finish(0)
        for t in range(1, Y):
            remote(gram.at[rows], gram.at[rows], g_send.at[0], g_recv.at[0], (y_peers[t], c)).start()

    def gram_x():
        arrived(yr.at[0], g_recv.at[0])
        rows = pl.ds(pl.multiple_of(x * 64, 64), 64)
        for t in range(1, X):
            remote(gram.at[rows], gram.at[rows], g_send.at[1], g_recv.at[1], (x_peers[t], c)).start()

    def gram_finish():
        arrived(xr.at[0], g_recv.at[1])
        table[:, :S] = gram[...]
        square = (S, S)
        table[:, S:] = jnp.where(
            lax.broadcasted_iota(jnp.int32, square, 0) == lax.broadcasted_iota(jnp.int32, square, 1), 1.0, 0.0
        ).astype(F32)

    def unit_of(p):
        return (last_ys, pl.ds(pl.multiple_of(core * HALF, HALF), HALF)) if p == LAST else (ys.at[p], slice(None))

    def place(p):
        low, high = PAIRS[p]
        if p == LAST:
            unit, lanes_of, rows_of, lane_sem = y * X + x, low, high, core
        else:
            unit, lane_sem = x * Y + y, 0
            lanes_of = jnp.where(core == 0, low, high)
            rows_of = jnp.where(core == 0, high, low)
        group = lax.rem(c + lanes_of + Z, Z)
        number = lax.rem(c + rows_of + Z, Z) * 32 + unit
        owner, slot = lax.div(number, 6), lax.rem(number, 6)
        return group, owner, slot, lane_sem

    def to_owner(p):
        group, owner, slot, lane_sem = place(p)
        unit, lanes = unit_of(p)
        rows = pl.ds(pl.multiple_of(slot * 8, 8), 8)
        mine = jnp.logical_and(owner == s, group == c)
        copy = remote(unit, fin.at[rows, lanes], f_send.at[p, 0], f_recv.at[slot, lane_sem], (owner, group))
        return mine, rows, copy

    def to_ahead(p):
        group, owner, slot, lane_sem = place(p)
        unit, lanes = unit_of(p)
        ahead = lax.rem(owner + SPACE - 1, SPACE)
        mine = jnp.logical_and(ahead == s, group == c)
        copy = remote(unit, fin.at[48:56, lanes], f_send.at[p, 1], f_recv.at[6, lane_sem], (ahead, group))
        return slot == 0, mine, copy

    def deliver(p):
        unit, _ = unit_of(p)
        unit[...] = finish(p)
        mine, rows, copy = to_owner(p)
        first, mine_ahead, copy_ahead = to_ahead(p)

        @pl.when(jnp.logical_not(mine))
        def _():
            copy.start()

        @pl.when(jnp.logical_and(first, jnp.logical_not(mine_ahead)))
        def _():
            copy_ahead.start()

        if p == 1:

            @pl.when(mine)
            def _():
                fin[rows] = unit[...]

            @pl.when(jnp.logical_and(first, mine_ahead))
            def _():
                fin[48:56] = unit[...]

    def sent(p):
        mine, _, copy = to_owner(p)

        @pl.when(jnp.logical_not(mine))
        def _():
            copy.wait_send()

        first, mine_ahead, copy_ahead = to_ahead(p)

        @pl.when(jnp.logical_and(first, jnp.logical_not(mine_ahead)))
        def _():
            copy_ahead.wait_send()

    def collect(slot):
        number = lax.rem(s * 6 + slot, SPACE * 6)
        apart = lax.rem(lax.div(number, 32) - c + Z, Z)
        within = lax.rem(number, 32)
        near = apart <= Z // 2
        home = jnp.where(near, lax.div(apart, 2), Z - lax.div(Z - apart + 1, 2))
        source = at(lax.rem(within, Y), lax.div(within, Y), jnp.where(near, 0, 1))
        own = jnp.logical_and(source == s, lax.rem(home, Z) == 0)
        rows = slice(slot * 8, slot * 8 + 8)

        @pl.when(apart == 0)
        def _():
            fin[rows] = gram[pl.ds(pl.multiple_of(within * 8, 8), 8)]

        @pl.when(apart == Z // 2)
        def _():
            arrived(fin.at[rows, :HALF], f_recv.at[slot, 0])
            arrived(fin.at[rows, HALF:], f_recv.at[slot, 1])

        whole = jnp.logical_and(apart != 0, apart != Z // 2)

        @pl.when(jnp.logical_and(whole, jnp.logical_not(own)))
        def _():
            arrived(fin.at[rows], f_recv.at[slot, 0])

    one, two, three = ORDER
    features(one)
    enter()
    hop(1, one)
    halo_landed()
    features(two)
    hop(1, two)
    features(three)
    hop(1, three)
    multiply(0, ORDER)
    core_start(0)
    first_stage(0)
    landed(1, one)
    hop(2, one)
    second_stage(0)
    landed(1, two)
    hop(2, two)
    gram_y()
    landed(1, three)
    hop(2, three)
    gram_x()
    multiply(1, ORDER)
    core_start(1)
    multiply(2, ORDER)
    core_start(2)
    landed(2, one)
    hop(3, one)
    gram_finish()
    first_stage(1)
    factor_step(table, 0)
    landed(2, two)
    hop(3, two)
    first_stage(2)
    factor_step(table, 1)
    landed(2, three)
    hop(3, three)
    multiply(3, ORDER)
    core_start(3)
    multiply(4, ORDER)
    core_start(4)
    second_stage(1)
    second_stage(2)
    factor_step(table, 2)
    landed(3, one)
    multiply(5, (one,))
    multiply(6, (one,))
    first_stage(3)
    factor_step(table, 3)
    deliver(1)
    deliver(2)
    landed(3, two)
    multiply(5, (two,))
    multiply(6, (two,))
    first_stage(4)
    landed(3, three)
    multiply(5, (three,))
    core_start(5)
    multiply(6, (three,))
    core_start(6)
    second_stage(3)
    second_stage(4)
    first_stage(5)
    first_stage(6)
    second_stage(5)
    second_stage(6)
    deliver(3)
    deliver(4)
    deliver(5)
    deliver(6)

    @pl.when(s < SPACE - 1)
    def _():
        to_right.wait_send()

    @pl.when(s > 0)
    def _():
        to_left.wait_send()

    for way in range(2):
        arrived(xt.at[0:REACH], z_send.at[way])
    arrived(yr.at[0], g_send.at[0])
    arrived(xr.at[0], g_send.at[1])
    for p in range(LAST + 1):
        arrived(core_refs(p)[2], c_send.at[p])
        for (_, _, _, send, _), landing, _, _ in stages(p):
            arrived(landing, send)
        if p > 0:
            sent(p)

    for slot in range(7):
        collect(slot)
    out_ref[...] = exact_dot(fin[1:49], table[:, S:], NT)


def body(velocity, metric):
    cells, pairs = velocity.shape[1], len(PAIRS)
    dma = pltpu.SemaphoreType.DMA
    tiles = pl.pallas_call(
        kernel,
        out_shape=jax.ShapeDtypeStruct((3072 // SPACE, S), F32),
        in_specs=[pl.BlockSpec(memory_space=pl.ANY)] * 2,
        out_specs=pl.BlockSpec(memory_space=pltpu.VMEM),
        scratch_shapes=[
            pltpu.VMEM((3, cells, S), jnp.bfloat16),
            pltpu.VMEM((cells,), F32),
            pltpu.VMEM((2 * REACH + 1, 3, S, cells), jnp.bfloat16),
            pltpu.VMEM((2, 3, 16, S), jnp.bfloat16),
            pltpu.VMEM((pairs - 1, 2, S, S), F32),
            pltpu.VMEM((pairs - 1, S, S), F32),
            pltpu.VMEM((pairs - 1, S, S), F32),
            pltpu.VMEM((pairs - 1, X - 1, S // X, S), F32),
            pltpu.VMEM((pairs - 1, S // X, S), F32),
            pltpu.VMEM((pairs - 1, Y - 1, 8, S), F32),
            pltpu.VMEM((pairs - 1, 8, S), F32),
            pltpu.VMEM((2, S, HALF), F32),
            pltpu.VMEM((S, HALF), F32),
            pltpu.VMEM((S, HALF), F32),
            pltpu.VMEM((Y - 1, S // Y, HALF), F32),
            pltpu.VMEM((S // Y, HALF), F32),
            pltpu.VMEM((X - 1, 8, HALF), F32),
            pltpu.VMEM((8, HALF), F32),
            pltpu.VMEM((S, S), F32),
            pltpu.VMEM((S, 2 * S), F32),
            pltpu.VMEM((56, S), F32),
            dma((2,)), dma((2,)), dma((2,)), dma((2,)), dma((2, REACH, 3)),
            dma((pairs,)), dma((pairs, Y)), dma((pairs,)), dma((pairs,)), dma((pairs,)), dma((pairs,)),
            dma((2,)), dma((2,)), dma((pairs, 2)), dma((7, 2)),
        ],
        compiler_params=pltpu.CompilerParams(
            collective_id=0, has_side_effects=True, vmem_limit_bytes=56 * 1024 * 1024
        ),
    )(velocity, metric)
    return tiles.T


def solution(mesh):
    in_specs = (P(None, "space", "tm"), P("space"))
    out_specs = P("tm", "space")
    return jax.shard_map(body, mesh=mesh, in_specs=in_specs, out_specs=out_specs, check_vma=False)
```

```python
import jax
import jax.numpy as jnp
from jax import lax
from jax.experimental import pallas as pl
from jax.experimental.pallas import tpu as pltpu
from jax.sharding import PartitionSpec as P

MESH = pl.DeviceIdType.MESH
X, Y, Z = 4, 8, 12
SPACE = 2 * X * Y
S = 256
PAIRS = ((0, 0), (0, 1), (-1, 1), (-1, 2), (-2, 2), (-2, 3), (-3, 3))
LAST = len(PAIRS) - 1
REACH = 3
THIRD = 128
HALF = S // 2
ORDER = (1, 0, 2)
BLOCK = 64
WIDTH = 8
NT = (((1,), (1,)), ((), ()))
NN = (((1,), (0,)), ((), ()))
F32 = jnp.float32


def exact_dot(left, right, dims):
    return lax.dot_general(
        left, right, dims, precision=lax.Precision.HIGHEST, preferred_element_type=F32
    )


def eliminate(work):
    below = lax.broadcasted_iota(jnp.int32, work.shape, 0)
    for first in range(0, BLOCK, WIDTH):
        columns = [jnp.broadcast_to(work[:, k : k + 1], work.shape) for k in range(first, first + WIDTH)]
        rows = [work[k : k + 1, :] for k in range(first, first + WIDTH)]
        scales = []
        for t in range(WIDTH):
            k = first + t
            scale = jnp.where(below > k, columns[t] * (1.0 / columns[t][k : k + 1, :]), 0.0)
            scales.append(scale)
            for u in range(t + 1, WIDTH):
                columns[u] = columns[u] - scale * columns[u][k : k + 1, :]
                rows[u] = rows[u] - scale[first + u : first + u + 1, :] * rows[t]
        for scale, pivot_row in zip(scales, rows):
            work = work - scale * pivot_row
    return work


def factor_step(table, j):
    low = j * BLOCK
    rows = table[low : low + BLOCK, :]
    row_at = lax.broadcasted_iota(jnp.int32, (BLOCK, BLOCK), 0)
    lane_at = lax.broadcasted_iota(jnp.int32, (BLOCK, BLOCK), 1)
    eye = jnp.where(row_at == lane_at, 1.0, 0.0).astype(F32)
    work = eliminate(jnp.concatenate([rows[:, low : low + BLOCK], eye], axis=1))
    pivots = jnp.sum(jnp.where(row_at == lane_at, work[:, :BLOCK], 0.0), axis=1, keepdims=True)
    inverse = work[:, BLOCK:] / jnp.sqrt(pivots)
    solved = exact_dot(inverse, rows, NN)
    table[low : low + BLOCK, :] = solved
    if low + BLOCK < S:
        panel = jnp.transpose(solved[:, :S])[low + BLOCK :, :]
        table[low + BLOCK :, :] = table[low + BLOCK :, :] - exact_dot(panel, solved, NN)


def kernel(
    v_hbm, m_hbm, out_ref,
    v_ref, m_ref, xt, halo, part, cr, cs, xr, xs, yr, ys,
    last_part, last_cr, last_cs, last_yr, last_s, last_xr, last_ys, gram, table, fin,
    in_sem, halo_send, halo_recv, z_send, z_recv, c_send, c_recv, x_send, x_recv, y_send, y_recv,
    g_send, g_recv, f_send, f_recv,
):
    s = lax.axis_index("space")
    c = lax.axis_index("tm")
    core = lax.rem(s, 2)
    x = lax.rem(lax.div(s, 2), X)
    y = lax.div(s, 2 * X)
    plus, minus = lax.rem(c + 1, Z), lax.rem(c + Z - 1, Z)
    right, left = lax.rem(s + 1, SPACE), lax.rem(s + SPACE - 1, SPACE)
    cells = v_ref.shape[1]

    def at(y_at, x_at, core_at):
        return (y_at * X + x_at) * 2 + core_at

    partner = at(y, x, 1 - core)
    x_peers = [at(y, lax.rem(x + t, X), core) for t in range(X)]
    y_peers = [at(lax.rem(y + t, Y), x, core) for t in range(Y)]

    barrier = pltpu.get_barrier_semaphore()
    greeted = [(s, plus), (s, minus), (right, c), (left, c), (partner, c)]
    greeted += [(peer, c) for peer in x_peers[1:] + y_peers[1:]]
    for device in greeted:
        pl.semaphore_signal(barrier, inc=1, device_id=device, device_id_type=MESH)
    cuts = (0, THIRD - 16, 2 * THIRD + 16, cells)
    fetches = [
        pltpu.make_async_copy(v_hbm.at[:, low:high, :], v_ref.at[:, low:high, :], in_sem.at[i])
        for i, (low, high) in enumerate(zip(cuts, cuts[1:]))
    ]
    fetch_m = pltpu.make_async_copy(m_hbm, m_ref, in_sem.at[3])
    for fetch in (fetches[1], fetch_m, fetches[0], fetches[2]):
        fetch.start()
    fetches[1].wait()
    fetch_m.wait()

    def remote(src, dst, send, recv, device):
        return pltpu.make_async_remote_copy(
            src_ref=src, dst_ref=dst, send_sem=send, recv_sem=recv, device_id=device, device_id_type=MESH
        )

    def arrived(ref, sem):
        pltpu.make_async_copy(ref, ref, sem).wait()

    to_right = remote(v_ref.at[:, cells - 16 :, :], halo.at[0], halo_send.at[0], halo_recv.at[0], (right, c))
    to_left = remote(v_ref.at[:, :16, :], halo.at[1], halo_send.at[1], halo_recv.at[1], (left, c))

    def halo_start():
        fetches[0].wait()
        fetches[2].wait()

        @pl.when(s < SPACE - 1)
        def _():
            to_right.start()

        @pl.when(s > 0)
        def _():
            to_left.start()

    def halo_landed():
        @pl.when(s > 0)
        def _():
            to_right.wait_recv()

        @pl.when(s == 0)
        def _():
            halo[0] = jnp.zeros_like(halo[0])

        @pl.when(s < SPACE - 1)
        def _():
            to_left.wait_recv()

        @pl.when(s == SPACE - 1)
        def _():
            halo[1] = jnp.zeros_like(halo[1])

    row = lax.broadcasted_iota(jnp.int32, (THIRD, S), 0)

    def features(q):
        low = q * THIRD
        start, stop = max(low - 16, 0), min(low + THIRD + 16, cells)
        here = slice(low - start, low - start + THIRD)
        spacing = jnp.transpose(jnp.broadcast_to(m_ref[low : low + THIRD].reshape(1, THIRD), (THIRD, THIRD)))
        spacing = jnp.concatenate([spacing, spacing], axis=1)
        gradients = []
        for k in range(3):
            field = v_ref[k, start:stop].astype(F32)
            after = pltpu.roll(field, stop - start - 1, 0)[here]
            before = pltpu.roll(field, 1, 0)[here]
            if stop == cells:
                edge = jnp.broadcast_to(halo[1, k].astype(F32)[0:1, :], (THIRD, S))
                after = jnp.where(row == THIRD - 1, edge, after)
            if start == 0:
                edge = jnp.broadcast_to(halo[0, k].astype(F32)[15:16, :], (THIRD, S))
                before = jnp.where(row == 0, edge, before)
            gradients.append(spacing * (after - before) * 0.5)
        center = [v_ref[k, low : low + THIRD].astype(F32) for k in range(2)]
        gradients[2] = gradients[2] + center[0] * gradients[1] - center[1] * gradients[0]
        for k in range(3):
            xt[REACH, q, :, k * THIRD : (k + 1) * THIRD] = jnp.transpose(gradients[k]).astype(jnp.bfloat16)

    def hop(t, q):
        for way, device, sign in ((0, plus, -1), (1, minus, 1)):
            remote(
                xt.at[REACH + sign * (t - 1), q], xt.at[REACH + sign * t, q],
                z_send.at[way], z_recv.at[way, t - 1, q], (s, device),
            ).start()

    def landed(t, q):
        for way, sign in ((0, -1), (1, 1)):
            arrived(xt.at[REACH + sign * t, q], z_recv.at[way, t - 1, q])

    def gather(ref, at_index, term, q):
        ref[at_index] = term if q == ORDER[0] else ref[at_index] + term

    def multiply(p, thirds):
        low, high = PAIRS[p]
        for q in thirds:
            lower, upper = xt[REACH + low, q], xt[REACH + high, q]
            term = lax.dot_general(upper, lower, NT, preferred_element_type=F32)
            if p == LAST:
                gather(last_part, 0, term[:, :HALF], q)
                gather(last_part, 1, term[:, HALF:], q)
                continue
            gather(part, (p, 0), term, q)
            if p > 0:
                gather(part, (p, 1), lax.dot_general(lower, upper, NT, preferred_element_type=F32), q)

    def stages(p):
        x_axis = (x, x_peers, X, x_send.at[p], x_recv.at[p])
        y_axis = (y, y_peers, Y, y_send.at[p], y_recv.at[p])
        if p == LAST:
            return (y_axis, last_yr, last_s, S // Y), (x_axis, last_xr, last_s, 8)
        return (x_axis, xr.at[p], xs.at[p], S // X), (y_axis, yr.at[p], xs.at[p], 8)

    def core_refs(p):
        if p == LAST:
            return last_part.at[core], last_part.at[1 - core], last_cr, last_cs
        if p == 0:
            return part.at[0, 0], part.at[0, 0], cr.at[0], cs.at[0]
        return part.at[p, core], part.at[p, 1 - core], cr.at[p], cs.at[p]

    def piece(p, t):
        (at_axis, _, count, _, _), _, _, size = stages(p)[0]
        return pl.ds(pl.multiple_of(lax.rem(at_axis + t, count) * size, size), size)

    def farthest_first(count):
        return list(range(1, count))

    def order(p):
        return farthest_first(stages(p)[0][0][2]) + [0]

    def core_copy(p, t):
        _, given, landing, _ = core_refs(p)
        rows = piece(p, t)
        return remote(given.at[rows], landing.at[rows], c_send.at[p], c_recv.at[p, t], (partner, c))

    def core_start(p):
        for t in order(p):
            core_copy(p, t).start()

    def first_stage(p):
        (_, peers, _, send, recv), landing, _, _ = stages(p)[0]
        kept, _, received, summed = core_refs(p)
        for t in order(p):
            core_copy(p, t).wait_recv()
            rows = piece(p, t)
            summed[rows] = kept[rows] + received[rows]
            if t > 0:
                remote(summed.at[rows], landing.at[t - 1], send, recv, (peers[t], c)).start()

    def second_stage(p):
        (_, _, count, _, recv), landing, summed, _ = stages(p)[0]
        (at_axis, peers, others, send, recv_next), landing_next, _, size = stages(p)[1]
        arrived(landing, recv)
        total = core_refs(p)[3][piece(p, 0)]
        for t in range(count - 1):
            total = total + landing[t]
        summed[...] = total
        for t in farthest_first(others):
            chunk = pl.ds(pl.multiple_of(lax.rem(at_axis + t, others) * size, size), size)
            remote(summed.at[chunk], landing_next.at[t - 1], send, recv_next, (peers[t], c)).start()

    def finish(p):
        (at_axis, _, count, _, recv), landing, summed, size = stages(p)[1]
        arrived(landing, recv)
        total = summed[pl.ds(pl.multiple_of(at_axis * size, size), size)]
        for t in range(count - 1):
            total = total + landing[t]
        return total

    def gram_y():
        rows = pl.ds(pl.multiple_of(x * 64 + y * 8, 8), 8)
        gram[rows] = finish(0)
        for t in range(1, Y):
            remote(gram.at[rows], gram.at[rows], g_send.at[0], g_recv.at[0], (y_peers[t], c)).start()

    def gram_x():
        arrived(yr.at[0], g_recv.at[0])
        rows = pl.ds(pl.multiple_of(x * 64, 64), 64)
        for t in range(1, X):
            remote(gram.at[rows], gram.at[rows], g_send.at[1], g_recv.at[1], (x_peers[t], c)).start()

    def gram_finish():
        arrived(xr.at[0], g_recv.at[1])
        table[:, :S] = gram[...]
        square = (S, S)
        table[:, S:] = jnp.where(
            lax.broadcasted_iota(jnp.int32, square, 0) == lax.broadcasted_iota(jnp.int32, square, 1), 1.0, 0.0
        ).astype(F32)

    def unit_of(p):
        return (last_ys, pl.ds(pl.multiple_of(core * HALF, HALF), HALF)) if p == LAST else (ys.at[p], slice(None))

    def place(p):
        low, high = PAIRS[p]
        if p == LAST:
            unit, lanes_of, rows_of, lane_sem = y * X + x, low, high, core
        else:
            unit, lane_sem = x * Y + y, 0
            lanes_of = jnp.where(core == 0, low, high)
            rows_of = jnp.where(core == 0, high, low)
        group = lax.rem(c + lanes_of + Z, Z)
        number = lax.rem(c + rows_of + Z, Z) * 32 + unit
        owner, slot = lax.div(number, 6), lax.rem(number, 6)
        return group, owner, slot, lane_sem

    places = {p: place(p) for p in range(1, LAST + 1)}

    def to_owner(p):
        group, owner, slot, lane_sem = places[p]
        unit, lanes = unit_of(p)
        rows = pl.ds(pl.multiple_of(slot * 8, 8), 8)
        mine = jnp.logical_and(owner == s, group == c)
        copy = remote(unit, fin.at[rows, lanes], f_send.at[p, 0], f_recv.at[slot, lane_sem], (owner, group))
        return mine, rows, copy

    def to_ahead(p):
        group, owner, slot, lane_sem = places[p]
        unit, lanes = unit_of(p)
        ahead = lax.rem(owner + SPACE - 1, SPACE)
        mine = jnp.logical_and(ahead == s, group == c)
        copy = remote(unit, fin.at[48:56, lanes], f_send.at[p, 1], f_recv.at[6, lane_sem], (ahead, group))
        return slot == 0, mine, copy

    def deliver(p):
        unit, _ = unit_of(p)
        unit[...] = finish(p)
        mine, rows, copy = to_owner(p)
        first, mine_ahead, copy_ahead = to_ahead(p)

        @pl.when(jnp.logical_not(mine))
        def _():
            copy.start()

        @pl.when(jnp.logical_and(first, jnp.logical_not(mine_ahead)))
        def _():
            copy_ahead.start()

        if p == 1:

            @pl.when(mine)
            def _():
                fin[rows] = unit[...]

            @pl.when(jnp.logical_and(first, mine_ahead))
            def _():
                fin[48:56] = unit[...]

    def sent(p):
        mine, _, copy = to_owner(p)

        @pl.when(jnp.logical_not(mine))
        def _():
            copy.wait_send()

        first, mine_ahead, copy_ahead = to_ahead(p)

        @pl.when(jnp.logical_and(first, jnp.logical_not(mine_ahead)))
        def _():
            copy_ahead.wait_send()

    def origin(slot):
        number = lax.rem(s * 6 + slot, SPACE * 6)
        apart = lax.rem(lax.div(number, 32) - c + Z, Z)
        within = lax.rem(number, 32)
        near = apart <= Z // 2
        home = jnp.where(near, lax.div(apart, 2), Z - lax.div(Z - apart + 1, 2))
        source = at(lax.rem(within, Y), lax.div(within, Y), jnp.where(near, 0, 1))
        own = jnp.logical_and(source == s, lax.rem(home, Z) == 0)
        return apart, within, own

    origins = [origin(slot) for slot in range(7)]

    def collect(slot):
        apart, within, own = origins[slot]
        rows = slice(slot * 8, slot * 8 + 8)

        @pl.when(apart == 0)
        def _():
            fin[rows] = gram[pl.ds(pl.multiple_of(within * 8, 8), 8)]

        @pl.when(apart == Z // 2)
        def _():
            arrived(fin.at[rows, :HALF], f_recv.at[slot, 0])
            arrived(fin.at[rows, HALF:], f_recv.at[slot, 1])

        whole = jnp.logical_and(apart != 0, apart != Z // 2)

        @pl.when(jnp.logical_and(whole, jnp.logical_not(own)))
        def _():
            arrived(fin.at[rows], f_recv.at[slot, 0])

    one, two, three = ORDER
    features(one)
    pl.semaphore_wait(barrier, len(greeted))
    hop(1, one)
    halo_start()
    halo_landed()
    features(two)
    hop(1, two)
    features(three)
    hop(1, three)
    multiply(0, ORDER)
    core_start(0)
    first_stage(0)
    landed(1, one)
    hop(2, one)
    second_stage(0)
    landed(1, two)
    hop(2, two)
    gram_y()
    landed(1, three)
    hop(2, three)
    gram_x()
    multiply(1, ORDER)
    core_start(1)
    multiply(2, ORDER)
    core_start(2)
    landed(2, one)
    hop(3, one)
    gram_finish()
    first_stage(1)
    factor_step(table, 0)
    landed(2, two)
    hop(3, two)
    first_stage(2)
    factor_step(table, 1)
    landed(2, three)
    hop(3, three)
    multiply(3, ORDER)
    core_start(3)
    multiply(4, ORDER)
    core_start(4)
    second_stage(1)
    second_stage(2)
    factor_step(table, 2)
    landed(3, one)
    multiply(5, (one,))
    multiply(6, (one,))
    first_stage(3)
    factor_step(table, 3)
    deliver(1)
    deliver(2)
    landed(3, two)
    multiply(5, (two,))
    multiply(6, (two,))
    first_stage(4)
    landed(3, three)
    multiply(5, (three,))
    core_start(5)
    multiply(6, (three,))
    core_start(6)
    second_stage(3)
    second_stage(4)
    first_stage(5)
    first_stage(6)
    second_stage(5)
    second_stage(6)
    deliver(3)
    deliver(4)
    deliver(5)
    deliver(6)

    @pl.when(s < SPACE - 1)
    def _():
        to_right.wait_send()

    @pl.when(s > 0)
    def _():
        to_left.wait_send()

    for way in range(2):
        arrived(xt.at[0:REACH], z_send.at[way])
    arrived(yr.at[0], g_send.at[0])
    arrived(xr.at[0], g_send.at[1])
    for p in range(LAST + 1):
        arrived(core_refs(p)[2], c_send.at[p])
        for (_, _, _, send, _), landing, _, _ in stages(p):
            arrived(landing, send)
        if p > 0:
            sent(p)

    for slot in range(7):
        collect(slot)
    out_ref[...] = exact_dot(fin[1:49], table[:, S:], NT)


def body(velocity, metric):
    cells, pairs = velocity.shape[1], len(PAIRS)
    dma = pltpu.SemaphoreType.DMA
    tiles = pl.pallas_call(
        kernel,
        out_shape=jax.ShapeDtypeStruct((3072 // SPACE, S), F32),
        in_specs=[pl.BlockSpec(memory_space=pl.ANY)] * 2,
        out_specs=pl.BlockSpec(memory_space=pltpu.VMEM),
        scratch_shapes=[
            pltpu.VMEM((3, cells, S), jnp.bfloat16),
            pltpu.VMEM((cells,), F32),
            pltpu.VMEM((2 * REACH + 1, 3, S, cells), jnp.bfloat16),
            pltpu.VMEM((2, 3, 16, S), jnp.bfloat16),
            pltpu.VMEM((pairs - 1, 2, S, S), F32),
            pltpu.VMEM((pairs - 1, S, S), F32),
            pltpu.VMEM((pairs - 1, S, S), F32),
            pltpu.VMEM((pairs - 1, X - 1, S // X, S), F32),
            pltpu.VMEM((pairs - 1, S // X, S), F32),
            pltpu.VMEM((pairs - 1, Y - 1, 8, S), F32),
            pltpu.VMEM((pairs - 1, 8, S), F32),
            pltpu.VMEM((2, S, HALF), F32),
            pltpu.VMEM((S, HALF), F32),
            pltpu.VMEM((S, HALF), F32),
            pltpu.VMEM((Y - 1, S // Y, HALF), F32),
            pltpu.VMEM((S // Y, HALF), F32),
            pltpu.VMEM((X - 1, 8, HALF), F32),
            pltpu.VMEM((8, HALF), F32),
            pltpu.VMEM((S, S), F32),
            pltpu.VMEM((S, 2 * S), F32),
            pltpu.VMEM((56, S), F32),
            dma((4,)), dma((2,)), dma((2,)), dma((2,)), dma((2, REACH, 3)),
            dma((pairs,)), dma((pairs, Y)), dma((pairs,)), dma((pairs,)), dma((pairs,)), dma((pairs,)),
            dma((2,)), dma((2,)), dma((pairs, 2)), dma((7, 2)),
        ],
        compiler_params=pltpu.CompilerParams(
            collective_id=0, has_side_effects=True, vmem_limit_bytes=56 * 1024 * 1024
        ),
    )(velocity, metric)
    return tiles.T


def solution(mesh):
    in_specs = (P(None, "space", "tm"), P("space"))
    out_specs = P("tm", "space")
    return jax.shard_map(body, mesh=mesh, in_specs=in_specs, out_specs=out_specs, check_vma=False)
```
